256 devices in a mesh: row: 8 (over y, core), col: 32 (over z, x).
Axes of the slice: x: 4, y: 4, z: 8, core: 2. Of those that a mesh axis runs over, the one named last changes fastest.
Arguments:
- block_values: bfloat16 [8, 32, 24, 256, 256], P('row', 'col'), may hold values from -0.078125 to 0.078125
- block_rows: int32 [8, 32, 24], P('row', 'col'), may hold values from 0 to 7, as said below
- block_cols: int32 [8, 32, 24], P('row', 'col'), may hold values from 0 to 7
- block_count: int32 [8, 32], P('row', 'col'), may hold values from 8 to 24, as said below
- basis: bfloat16 [65536, 256], P(('col', 'row')), may hold values from -6 to 6
Outputs:
- sweep_out: float32 [65536, 256], P(('col', 'row'))
The draws below stay inside these ranges and needn't reach their ends.
Inputs may be any that keep to these rules, and one draw needn't show every extreme that they name: Within one device all slots give distinct (block_rows, block_cols) pairs; slots at or beyond block_count hold no block. `block_count`: some device holds exactly 24 live slots.
All inputs are finite; a program needn't handle non-finite values.
Results may differ from the reference program's by a relative error of at most 0.0026.
Values may be sent and summed in bfloat16 or wider, within the bound.
No kernel may reach another device: no remote copies, remote signals or barrier semaphores. Data moves between devices by JAX's collectives and lax.ppermute only.
A program may use at most 64 MiB of HBM per device.

```python
import jax
import jax.numpy as jnp
from jax import lax

BS = 256
RANK = 256
RB = 8
CB = 8
BMAX = 24
COLS = 65536
N_ROW = 8
N_COL = 32


def block_pattern(key):
    base = jax.random.fold_in(key, 11)
    perm_key, count_key, pick_key, top_key = jax.random.split(base, 4)
    device_total = N_ROW * N_COL
    keys = jax.random.split(perm_key, device_total)
    orders = jax.vmap(lambda one_key: jax.random.permutation(one_key, RB * CB))(keys)[:, :BMAX]
    lowest = max(1, BMAX // 3)
    spread = BMAX - lowest
    first = jax.random.randint(count_key, (device_total,), 0, spread + 1)
    second = jax.random.randint(pick_key, (device_total,), 0, spread + 1)
    counts = lowest + first * second // max(spread, 1)
    busiest = jax.random.randint(top_key, (), 0, device_total)
    counts = jnp.where(jnp.arange(device_total) == busiest, BMAX, counts)
    return (orders.astype(jnp.int32).reshape(N_ROW, N_COL, BMAX), counts.astype(jnp.int32).reshape(N_ROW, N_COL))


def draw_block_rows(key, part):
    orders, counts = block_pattern(key)
    return (orders // CB).astype(jnp.int32)


def draw_block_cols(key, part):
    orders, counts = block_pattern(key)
    return (orders % CB).astype(jnp.int32)


def draw_block_count(key, part):
    orders, counts = block_pattern(key)
    return counts


def shard_levels(stream_key, shape, cuts, smallest, top_value):
    def one(dim, parts):
        draws = jax.random.uniform(jax.random.fold_in(jax.random.fold_in(stream_key, 6), dim), (parts,), jnp.float32, smallest / len(cuts), top_value / len(cuts))
        return jnp.repeat(jnp.exp(draws), shape[dim] // parts).reshape((-1,) + (1,) * (len(shape) - dim - 1))

    gain = one(*cuts[0])
    for cut in cuts[1:]:
        gain = gain * one(*cut)
    return gain


def noise(own_key, dims, scale, reach, cuts=(), kind=jnp.bfloat16):
    entries = jax.random.normal(own_key, dims, jnp.float32) * scale
    if len(cuts) > 0:
        entries = shard_levels(own_key, dims, cuts, -0.22, 0.18) * entries
    return jnp.clip(entries, min=-reach, max=reach).astype(kind)


def setup_inputs(seed: int = 0) -> dict:
    streams_of = jax.random.split(jax.random.key(seed), 6)
    return {
        "block_values": noise(streams_of[0], (N_ROW, N_COL, BMAX, BS, BS), (BS * BMAX) ** -0.5, 0.078125, ((0, 8), (1, 32))),
        "block_rows": draw_block_rows(jax.random.fold_in(streams_of[5], 71), 0),
        "block_cols": draw_block_cols(jax.random.fold_in(streams_of[5], 71), 0),
        "block_count": draw_block_count(jax.random.fold_in(streams_of[5], 71), 0),
        "basis": noise(streams_of[4], (COLS, RANK), 1.0, 6.0, ((0, 256),)),
    }


def sweep(tiles, total_out, all_blocks, source_ids, target_ids, all_counts, forward):
    device_total = N_ROW * N_COL
    device_ids = jnp.arange(device_total, dtype=jnp.int32)
    slot_index = jnp.arange(BMAX, dtype=jnp.int32)
    if forward:
        in_count, out_count, form = CB, RB, "bij,bjk->bik"
    else:
        in_count, out_count, form = RB, CB, "bji,bjk->bik"

    def visit(accum, item):
        blocks, source, target, live_count, device = item
        row_index = (device // N_COL).astype(jnp.int32)
        col_index = (device % N_COL).astype(jnp.int32)
        if forward:
            in_start, out_start = col_index * CB, row_index * RB
        else:
            in_start, out_start = row_index * RB, col_index * CB
        local_in = lax.dynamic_slice_in_dim(tiles, in_start, in_count, 0)
        picked = jnp.take(local_in, source, axis=0).astype(jnp.float32)
        products = jnp.einsum(form, blocks.astype(jnp.float32), picked, precision=lax.Precision.HIGHEST)
        live_mask = (slot_index < live_count).astype(jnp.float32)
        selector = (target[:, None] == jnp.arange(out_count, dtype=jnp.int32)[None, :]).astype(jnp.float32) * live_mask[:, None]
        added = jnp.einsum("bo,bik->oik", selector, products, precision=lax.Precision.HIGHEST)
        current = lax.dynamic_slice_in_dim(accum, out_start, out_count, 0)
        accum = lax.dynamic_update_slice_in_dim(accum, current + added, out_start, 0)
        return accum, None

    zero_acc = jnp.zeros((total_out, BS, RANK), jnp.float32)
    return lax.scan(visit, zero_acc, (all_blocks, source_ids, target_ids, all_counts, device_ids))[0]


def reference(block_values, block_rows, block_cols, block_count, basis):
    device_total = N_ROW * N_COL
    all_blocks = block_values.reshape(device_total, BMAX, BS, BS)
    all_rows = block_rows.reshape(device_total, BMAX)
    all_cols = block_cols.reshape(device_total, BMAX)
    all_counts = block_count.reshape(device_total)
    basis_tiles = basis.reshape(N_COL * CB, BS, RANK)
    row_sums = sweep(basis_tiles, N_ROW * RB, all_blocks, all_cols, all_rows, all_counts, True)
    row_basis = row_sums.astype(jnp.bfloat16)
    column_sums = sweep(row_basis, N_COL * CB, all_blocks, all_rows, all_cols, all_counts, False)
    return column_sums.reshape(N_COL * CB * BS, RANK)
```

```python
import functools

import jax
import jax.numpy as jnp
from jax import lax
from jax.experimental import pallas as pl
from jax.experimental.pallas import tpu as pltpu
from jax.sharding import PartitionSpec as P

BF16 = jnp.bfloat16
F32 = jnp.float32
F16 = jnp.float16
CORES = 2
NX = 4
SCALE_X = 64.0
SCALE_Z = 16.0


def shift_y(count, d):
    ny = count // CORES
    return [(y * CORES + k, (y + d) % ny * CORES + k) for y in range(ny) for k in range(CORES)]


def swap_core(count):
    return [(i, i ^ 1) for i in range(count)]


def shift_x(count, d):
    return [(i, i // NX * NX + (i % NX + d) % NX) for i in range(count)]


def z_groups(count):
    return [[z * NX + x for z in range(count // NX)] for x in range(NX)]


def vmem(n):
    return [pl.BlockSpec(memory_space=pltpu.VMEM)] * n


def smem(n):
    return [pl.BlockSpec(memory_space=pltpu.SMEM)] * n


def forward_kernel(rows, cols, count, blocks, *refs):
    pieces, (own, *sends), (basis, acc) = refs[:8], refs[8:12], refs[12:]
    y, k = lax.axis_index("row") // CORES, lax.axis_index("row") % CORES
    x = lax.axis_index("col") % NX
    for d in range(4):
        at = (y + 4 - d) % 4
        basis[at * CORES + k] = pieces[d][...]
        basis[at * CORES + 1 - k] = pieces[4 + d][...]
    acc[...] = jnp.zeros_like(acc)

    def visit(s, carry):
        r, c = rows[0, 0, s], cols[0, 0, s]
        acc[r] += jnp.dot(blocks[0, 0, s], basis[c], preferred_element_type=F32)
        return carry

    lax.fori_loop(0, count[0, 0], visit, 0)
    for h in range(2):
        own[h] = acc[x * 2 + h]
    for d in range(1, 4):
        to = (x + d) % NX
        for h in range(2):
            sends[d - 1][h] = acc[to * 2 + h] * SCALE_X


def backward_kernel(rows, cols, count, blocks, *refs):
    pieces, (own, send), (basis, acc) = refs[:4], refs[4:6], refs[6:]
    k = lax.axis_index("row") % CORES
    x = lax.axis_index("col") % NX
    for d in range(4):
        at = (x + 4 - d) % 4
        for h in range(2):
            basis[at * 2 + h] = pieces[d][h]
    acc[...] = jnp.zeros_like(acc)

    def visit(s, carry):
        r, c = rows[0, 0, s], cols[0, 0, s]
        acc[c] += lax.dot_general(
            blocks[0, 0, s], basis[r], (((0,), (0,)), ((), ())), preferred_element_type=F32
        )
        return carry

    lax.fori_loop(0, count[0, 0], visit, 0)
    for y in range(4):
        own[y] = acc[y * CORES + k]
        send[y] = acc[y * CORES + 1 - k].astype(send.dtype)


def call(kernel, outs, scratch, n_vmem, *args):
    return pl.pallas_call(
        kernel,
        out_shape=outs,
        in_specs=smem(3) + vmem(n_vmem),
        out_specs=vmem(len(outs)),
        scratch_shapes=scratch,
        compiler_params=pltpu.CompilerParams(vmem_limit_bytes=24 << 20),
    )(*args)


def body(block_values, block_rows, block_cols, block_count, basis):
    n_row, n_col = lax.axis_size("row"), lax.axis_size("col")
    size, rank = basis.shape
    table = (block_rows, block_cols, block_count)

    mine = [basis] + [lax.ppermute(basis, "row", shift_y(n_row, d)) for d in (1, 2, 3)]
    other = [lax.ppermute(p, "row", swap_core(n_row)) for p in mine]
    own, *sends = call(
        forward_kernel,
        [jax.ShapeDtypeStruct((2, size, rank), F32)] * 4,
        [pltpu.VMEM((8, size, rank), BF16), pltpu.VMEM((8, size, rank), F32)],
        9,
        *table, block_values, *mine, *other,
    )
    got = [lax.ppermute(s.astype(F16), "col", shift_x(n_col, d)) for d, s in zip((1, 2, 3), sends)]
    x_sum = own + (got[0].astype(F32) + got[1].astype(F32) + got[2].astype(F32)) * (1 / SCALE_X)
    nz = n_col // NX
    parts = (x_sum * SCALE_Z).astype(F16).reshape(nz, 2 * size // nz, rank)
    parts = lax.all_to_all(parts, "col", 0, 0, tiled=True, axis_index_groups=z_groups(n_col))
    share = (jnp.sum(parts.astype(F32), axis=0) * (1 / SCALE_Z)).astype(BF16)

    copies = jnp.broadcast_to(share[None], (nz, *share.shape))
    chunk = lax.all_to_all(copies, "col", 0, 0, tiled=True, axis_index_groups=z_groups(n_col))
    chunk = chunk.reshape(2, size, rank)
    chunks = [chunk] + [lax.ppermute(chunk, "col", shift_x(n_col, d)) for d in (1, 2, 3)]
    own, send = call(
        backward_kernel,
        [jax.ShapeDtypeStruct((4, size, rank), F32), jax.ShapeDtypeStruct((4, size, rank), BF16)],
        [pltpu.VMEM((8, size, rank), BF16), pltpu.VMEM((8, size, rank), F32)],
        5,
        *table, block_values, *chunks,
    )
    pair = own + lax.ppermute(send, "row", swap_core(n_row)).astype(F32)
    y = lax.axis_index("row") // CORES
    pick = lambda d: lax.dynamic_index_in_dim(pair, (y + d) % 4, 0, keepdims=False)
    got = [lax.ppermute(pick(d).astype(BF16), "row", shift_y(n_row, d)) for d in (1, 2, 3)]
    return pick(0) + got[0].astype(F32) + got[1].astype(F32) + got[2].astype(F32)


def solution(mesh):
    in_specs = (
        P("row", "col", None, None, None),
        P("row", "col", None),
        P("row", "col", None),
        P("row", "col"),
        P(("col", "row"), None),
    )
    out_specs = P(("col", "row"), None)
    return jax.shard_map(body, mesh=mesh, in_specs=in_specs, out_specs=out_specs, check_vma=False)
```

```python
import jax
import jax.numpy as jnp
from jax import lax
from jax.experimental import pallas as pl
from jax.experimental.pallas import tpu as pltpu
from jax.sharding import PartitionSpec as P

BF16 = jnp.bfloat16
F32 = jnp.float32
F16 = jnp.float16
CORES = 2
RING = 4
SCALE_X = 32.0
SCALE_Z = 16.0


def swap_core(v):
    return lax.ppermute(v, "row", [(i, i ^ 1) for i in range(lax.axis_size("row"))])


def swap_y(v, way):
    n = lax.axis_size("row")
    return lax.ppermute(v, "row", [(i, ring_partner(i // CORES, way) * CORES + i % CORES) for i in range(n)])


def swap_x(v, way):
    n = lax.axis_size("col")
    return lax.ppermute(v, "col", [(i, i // RING * RING + ring_partner(i % RING, way)) for i in range(n)])


def ring_partner(u, way):
    return u ^ 1 if way == "a" else 3 - u


def z_groups():
    n = lax.axis_size("col")
    return [[z * RING + x for z in range(n // RING)] for x in range(RING)]


def partners(u):
    return u + 1 - 2 * (u % 2), 3 - u, (u + 2) % RING


def fetch_kernel(blocks, basis, blocks_out, basis_out, sems):
    copies = [
        pltpu.make_async_copy(blocks, blocks_out, sems.at[0]),
        pltpu.make_async_copy(basis, basis_out, sems.at[1]),
    ]
    for copy in copies:
        copy.start()
    for copy in copies:
        copy.wait()


def fetch(blocks, basis):
    return pl.pallas_call(
        fetch_kernel,
        out_shape=[jax.ShapeDtypeStruct(blocks.shape, blocks.dtype), jax.ShapeDtypeStruct(basis.shape, basis.dtype)],
        in_specs=[pl.BlockSpec(memory_space=pltpu.HBM)] * 2,
        out_specs=[pl.BlockSpec(memory_space=pltpu.VMEM)] * 2,
        scratch_shapes=[pltpu.SemaphoreType.DMA((2,))],
        compiler_params=pltpu.CompilerParams(vmem_limit_bytes=16 << 20),
        cost_estimate=pl.CostEstimate(flops=0, bytes_accessed=8 << 20, transcendentals=0),
    )(blocks, basis)


def forward_kernel(table, count, blocks, *refs):
    pieces, (keep0, keep1, send_a, send_b), (basis, acc) = refs[:10], refs[10:14], refs[14:]
    half = basis.shape[1] // 2
    y, k = lax.axis_index("row") // CORES, lax.axis_index("row") % CORES
    x = lax.axis_index("col") % RING
    ya, yb, yo = partners(y)
    for core, group in ((k, pieces[:5]), (1 - k, pieces[5:])):
        for at, piece in zip((y, ya, yb), group[:3]):
            basis[at * CORES + core] = piece[...]
        basis[yo * CORES + core, :half] = group[3][...]
        basis[yo * CORES + core, half:] = group[4][...]
    acc[...] = jnp.zeros_like(acc)

    def visit(s, carry):
        r, c = table[s] // 8, table[s] % 8
        acc[r] += jnp.dot(blocks[0, 0, s], basis[c], preferred_element_type=F32)
        return carry

    lax.fori_loop(0, count[0, 0], visit, 0)
    xa, xb, xo = partners(x)
    keep0[0], keep0[1] = acc[2 * x], acc[2 * xb]
    keep1[0], keep1[1] = acc[2 * x + 1], acc[2 * xa + 1]
    send_a[0], send_a[1] = acc[2 * xa] * SCALE_X, acc[2 * xo] * SCALE_X
    send_b[0], send_b[1] = acc[2 * xb + 1] * SCALE_X, acc[2 * xo + 1] * SCALE_X


def backward_kernel(table, count, blocks, own, from_a, from_b, far0, far1, keep, send, basis, acc):
    y, k = lax.axis_index("row") // CORES, lax.axis_index("row") % CORES
    x = lax.axis_index("col") % RING
    xa, xb, xo = partners(x)
    for at, piece in zip((x, xa, xb), (own, from_a, from_b)):
        basis[2 * at], basis[2 * at + 1] = piece[0], piece[1]
    basis[2 * xo], basis[2 * xo + 1] = far0[0], far1[0]
    acc[...] = jnp.zeros_like(acc)

    def visit(s, carry):
        r, c = table[s] // 8, table[s] % 8
        acc[c] += lax.dot_general(
            blocks[0, 0, s], basis[r], (((0,), (0,)), ((), ())), preferred_element_type=F32
        )
        return carry

    lax.fori_loop(0, count[0, 0], visit, 0)
    for j in range(RING):
        keep[j] = acc[j * CORES + k]
        send[j] = acc[j * CORES + 1 - k].astype(send.dtype)


def pair_kernel(own, other, keep0, keep1, send_a, send_b):
    y = lax.axis_index("row") // CORES
    ya, yb, yo = partners(y)
    half = own.shape[1] // 2
    first, second = slice(0, half), slice(half, None)

    def both(at, rows):
        return own[at, rows] + other[at, rows].astype(F32)

    keep0[0], keep0[1] = both(y, first), both(yb, first)
    keep1[0], keep1[1] = both(y, second), both(ya, second)
    send_a[0], send_a[1] = both(ya, first).astype(BF16), both(yo, first).astype(BF16)
    send_b[0], send_b[1] = both(yb, second).astype(BF16), both(yo, second).astype(BF16)


def call(kernel, outs, scratch, n_smem, flops, *args):
    spec = pl.BlockSpec(memory_space=pltpu.VMEM)
    return pl.pallas_call(
        kernel,
        out_shape=[jax.ShapeDtypeStruct(shape, dtype) for shape, dtype in outs],
        in_specs=[pl.BlockSpec(memory_space=pltpu.SMEM)] * n_smem + [spec] * (len(args) - n_smem),
        out_specs=[spec] * len(outs),
        scratch_shapes=[pltpu.VMEM(shape, dtype) for shape, dtype in scratch],
        compiler_params=pltpu.CompilerParams(vmem_limit_bytes=24 << 20),
        cost_estimate=pl.CostEstimate(flops=flops, bytes_accessed=1 << 20, transcendentals=0),
    )(*args)


def body(block_values, block_rows, block_cols, block_count, basis):
    nz = lax.axis_size("col") // RING
    size, rank = basis.shape
    half = size // 2
    table = block_rows[0, 0] * 8 + block_cols[0, 0]
    flops = 2 * 24 * size * size * rank

    from_a, from_b = swap_y(basis, "a"), swap_y(basis, "b")
    blocks, mine = fetch(block_values, basis)
    from_a, from_b, blocks, mine = lax.optimization_barrier((from_a, from_b, blocks, mine))
    far0, far1 = swap_y(from_b[:half], "a"), swap_y(from_a[half:], "b")
    group = [from_a, from_b, far0, far1]
    other = [swap_core(basis)] + [swap_core(p) for p in group]

    two = (2, size, rank)
    keep0, keep1, send_a, send_b = call(
        forward_kernel, [(two, F32)] * 4, [((8, size, rank), BF16), ((8, size, rank), F32)], 2, flops,
        table, block_count, blocks, mine, *group, *other,
    )
    sum0 = keep0 + swap_x(send_a.astype(F16), "a").astype(F32) * (1 / SCALE_X)
    sum1 = keep1 + swap_x(send_b.astype(F16), "b").astype(F32) * (1 / SCALE_X)
    got0 = swap_x((sum0[1] * SCALE_Z).astype(F16), "b").astype(F32)
    got1 = swap_x((sum1[1] * SCALE_Z).astype(F16), "a").astype(F32)
    parts = jnp.concatenate([sum0[0] * SCALE_Z + got0, sum1[0] * SCALE_Z + got1], 0)
    parts = parts.astype(F16).reshape(nz, 2 * size // nz, rank)
    parts = lax.all_to_all(parts, "col", 0, 0, tiled=True, axis_index_groups=z_groups())
    share = (jnp.sum(parts.astype(F32), axis=0) * (1 / SCALE_Z)).astype(BF16)

    copies = jnp.broadcast_to(share[None], (nz, *share.shape))
    chunk = lax.all_to_all(copies, "col", 0, 0, tiled=True, axis_index_groups=z_groups()).reshape(two)
    from_a, from_b = swap_x(chunk, "a"), swap_x(chunk, "b")
    far0, far1 = swap_x(from_b[:1], "a"), swap_x(from_a[1:], "b")
    four = (RING, size, rank)
    keep, send = call(
        backward_kernel, [(four, F32), (four, BF16)], [((8, size, rank), BF16), ((8, size, rank), F32)], 2, flops,
        table, block_count, blocks, chunk, from_a, from_b, far0, far1,
    )
    part = (2, half, rank)
    keep0, keep1, send_a, send_b = call(
        pair_kernel, [(part, F32)] * 2 + [(part, BF16)] * 2, [], 0, 1 << 20, keep, swap_core(send)
    )
    sum0 = keep0 + swap_y(send_a, "a").astype(F32)
    sum1 = keep1 + swap_y(send_b, "b").astype(F32)
    out0 = sum0[0] + swap_y(sum0[1].astype(BF16), "b").astype(F32)
    out1 = sum1[0] + swap_y(sum1[1].astype(BF16), "a").astype(F32)
    return jnp.concatenate([out0, out1], 0)


def solution(mesh):
    in_specs = (
        P("row", "col", None, None, None),
        P("row", "col", None),
        P("row", "col", None),
        P("row", "col"),
        P(("col", "row"), None),
    )
    out_specs = P(("col", "row"), None)
    return jax.shard_map(body, mesh=mesh, in_specs=in_specs, out_specs=out_specs, check_vma=False)
```

```python
import functools

import jax
import jax.numpy as jnp
from jax import lax
from jax.experimental import pallas as pl
from jax.experimental.pallas import tpu as pltpu
from jax.sharding import PartitionSpec as P

BF16 = jnp.bfloat16
F32 = jnp.float32
F16 = jnp.float16
CORES = 2
NX = 4
UNROLL = 8
SCALE_X = 64.0
SCALE_Z = 16.0


def shift_y(count, d):
    ny = count // CORES
    return [(y * CORES + k, (y + d) % ny * CORES + k) for y in range(ny) for k in range(CORES)]


def swap_core(count):
    return [(i, i ^ 1) for i in range(count)]


def shift_x(count, d):
    return [(i, i // NX * NX + (i % NX + d) % NX) for i in range(count)]


def z_groups(count):
    return [[z * NX + x for z in range(count // NX)] for x in range(NX)]


def vmem(n):
    return [pl.BlockSpec(memory_space=pltpu.VMEM)] * n


def smem(n):
    return [pl.BlockSpec(memory_space=pltpu.SMEM)] * n


def fetch_kernel(blocks, basis, blocks_out, basis_out, sems):
    copies = [
        pltpu.make_async_copy(blocks, blocks_out, sems.at[0]),
        pltpu.make_async_copy(basis, basis_out, sems.at[1]),
    ]
    for copy in copies:
        copy.start()
    for copy in copies:
        copy.wait()


def fetch(blocks, basis):
    return pl.pallas_call(
        fetch_kernel,
        out_shape=[jax.ShapeDtypeStruct(blocks.shape, blocks.dtype), jax.ShapeDtypeStruct(basis.shape, basis.dtype)],
        in_specs=[pl.BlockSpec(memory_space=pltpu.HBM)] * 2,
        out_specs=[pl.BlockSpec(memory_space=pltpu.VMEM)] * 2,
        scratch_shapes=[pltpu.SemaphoreType.DMA((2,))],
        compiler_params=pltpu.CompilerParams(vmem_limit_bytes=16 << 20),
        cost_estimate=pl.CostEstimate(flops=0, bytes_accessed=8 << 20, transcendentals=0),
    )(blocks, basis)


def add_products(table, count, blocks, basis, acc, transposed):
    live, spare = count[0, 0], acc.shape[0] - 1
    acc[...] = jnp.zeros_like(acc)

    def visit(step, carry):
        products, targets = [], []
        for u in range(UNROLL):
            s = step * UNROLL + u
            r, c = table[s] // 8, table[s] % 8
            source, target, dim = (r, c, 0) if transposed else (c, r, 1)
            products.append(
                lax.dot_general(
                    blocks[0, 0, s], basis[source], (((dim,), (0,)), ((), ())), preferred_element_type=F32
                )
            )
            targets.append(jnp.where(s < live, target, spare))
        for target, product in zip(targets, products):
            acc[target] += product
        return carry

    lax.fori_loop(0, (live + UNROLL - 1) // UNROLL, visit, 0)


def forward_kernel(table, count, blocks, *refs):
    pieces, (own, *sends), (basis, acc) = refs[:8], refs[8:12], refs[12:]
    y, k = lax.axis_index("row") // CORES, lax.axis_index("row") % CORES
    x = lax.axis_index("col") % NX
    for d in range(4):
        at = (y + 4 - d) % 4
        basis[at * CORES + k] = pieces[d][...]
        basis[at * CORES + 1 - k] = pieces[4 + d][...]
    add_products(table, count, blocks, basis, acc, False)
    for h in range(2):
        own[h] = acc[x * 2 + h]
    for d in range(1, 4):
        to = (x + d) % NX
        for h in range(2):
            sends[d - 1][h] = acc[to * 2 + h] * SCALE_X


def backward_kernel(table, count, blocks, *refs):
    pieces, (own, send), (basis, acc) = refs[:4], refs[4:6], refs[6:]
    k = lax.axis_index("row") % CORES
    x = lax.axis_index("col") % NX
    for d in range(4):
        at = (x + 4 - d) % 4
        for h in range(2):
            basis[at * 2 + h] = pieces[d][h]
    add_products(table, count, blocks, basis, acc, True)
    for y in range(4):
        own[y] = acc[y * CORES + k]
        send[y] = acc[y * CORES + 1 - k].astype(send.dtype)


def call(kernel, outs, scratch, n_vmem, *args):
    flops = 2 * 24 * 256**3
    return pl.pallas_call(
        kernel,
        out_shape=outs,
        in_specs=smem(2) + vmem(n_vmem),
        out_specs=vmem(len(outs)),
        scratch_shapes=scratch,
        compiler_params=pltpu.CompilerParams(vmem_limit_bytes=28 << 20),
        cost_estimate=pl.CostEstimate(flops=flops, bytes_accessed=1 << 20, transcendentals=0),
    )(*args)


def body(block_values, block_rows, block_cols, block_count, basis):
    n_row, n_col = lax.axis_size("row"), lax.axis_size("col")
    size, rank = basis.shape
    table = (block_rows[0, 0] * 8 + block_cols[0, 0], block_count)

    mine = [basis] + [lax.ppermute(basis, "row", shift_y(n_row, d)) for d in (1, 2, 3)]
    blocks, own = fetch(block_values, basis)
    mine[1], blocks, own = lax.optimization_barrier((mine[1], blocks, own))
    other = [lax.ppermute(p, "row", swap_core(n_row)) for p in mine]
    own, *sends = call(
        forward_kernel,
        [jax.ShapeDtypeStruct((2, size, rank), F32)] * 4,
        [pltpu.VMEM((8, size, rank), BF16), pltpu.VMEM((9, size, rank), F32)],
        9,
        *table, blocks, own, *mine[1:], *other,
    )
    got = [lax.ppermute(s.astype(F16), "col", shift_x(n_col, d)) for d, s in zip((1, 2, 3), sends)]
    x_sum = own + (got[0].astype(F32) + got[1].astype(F32) + got[2].astype(F32)) * (1 / SCALE_X)
    nz = n_col // NX
    parts = (x_sum * SCALE_Z).astype(F16).reshape(nz, 2 * size // nz, rank)
    parts = lax.all_to_all(parts, "col", 0, 0, tiled=True, axis_index_groups=z_groups(n_col))
    share = (jnp.sum(parts.astype(F32), axis=0) * (1 / SCALE_Z)).astype(BF16)

    copies = jnp.broadcast_to(share[None], (nz, *share.shape))
    chunk = lax.all_to_all(copies, "col", 0, 0, tiled=True, axis_index_groups=z_groups(n_col))
    chunk = chunk.reshape(2, size, rank)
    chunks = [chunk] + [lax.ppermute(chunk, "col", shift_x(n_col, d)) for d in (1, 2, 3)]
    own, send = call(
        backward_kernel,
        [jax.ShapeDtypeStruct((4, size, rank), F32), jax.ShapeDtypeStruct((4, size, rank), BF16)],
        [pltpu.VMEM((8, size, rank), BF16), pltpu.VMEM((9, size, rank), F32)],
        5,
        *table, blocks, *chunks,
    )
    pair = own + lax.ppermute(send, "row", swap_core(n_row)).astype(F32)
    y = lax.axis_index("row") // CORES
    pick = lambda d: lax.dynamic_index_in_dim(pair, (y + d) % 4, 0, keepdims=False)
    got = [lax.ppermute(pick(d).astype(BF16), "row", shift_y(n_row, d)) for d in (1, 2, 3)]
    return pick(0) + got[0].astype(F32) + got[1].astype(F32) + got[2].astype(F32)


def solution(mesh):
    in_specs = (
        P("row", "col", None, None, None),
        P("row", "col", None),
        P("row", "col", None),
        P("row", "col"),
        P(("col", "row"), None),
    )
    out_specs = P(("col", "row"), None)
    return jax.shard_map(body, mesh=mesh, in_specs=in_specs, out_specs=out_specs, check_vma=False)
```

```python
import jax
import jax.numpy as jnp
from jax import lax
from jax.experimental import pallas as pl
from jax.experimental.pallas import tpu as pltpu
from jax.sharding import PartitionSpec as P

BF16 = jnp.bfloat16
F32 = jnp.float32
F16 = jnp.float16
CORES = 2
NX = 4
UNROLL = 8
SHIFTS_A, SHIFTS_B, SHIFTS_C, SHIFTS_D = (1, 3, 2), (1, 3, 2), (1, 3, 2), (1, 3, 2)
SCALE_X = 64.0
SCALE_Z = 16.0


def shift_y(count, d):
    ny = count // CORES
    return [(y * CORES + k, (y + d) % ny * CORES + k) for y in range(ny) for k in range(CORES)]


def swap_core(count):
    return [(i, i ^ 1) for i in range(count)]


def shift_x(count, d):
    return [(i, i // NX * NX + (i % NX + d) % NX) for i in range(count)]


def z_groups(count):
    return [[z * NX + x for z in range(count // NX)] for x in range(NX)]


def x_groups(count):
    return [[z * NX + x for x in range(NX)] for z in range(count // NX)]


def y_groups(count):
    return [[y * CORES + k for y in range(count // CORES)] for k in range(CORES)]


def vmem(n):
    return [pl.BlockSpec(memory_space=pltpu.VMEM)] * n


def smem(n):
    return [pl.BlockSpec(memory_space=pltpu.SMEM)] * n


def fetch_kernel(blocks, basis, blocks_out, basis_out, sems):
    copies = [
        pltpu.make_async_copy(blocks, blocks_out, sems.at[0]),
        pltpu.make_async_copy(basis, basis_out, sems.at[1]),
    ]
    for copy in copies:
        copy.start()
    for copy in copies:
        copy.wait()


def fetch(blocks, basis):
    return pl.pallas_call(
        fetch_kernel,
        out_shape=[jax.ShapeDtypeStruct(blocks.shape, blocks.dtype), jax.ShapeDtypeStruct(basis.shape, basis.dtype)],
        in_specs=[pl.BlockSpec(memory_space=pltpu.HBM)] * 2,
        out_specs=[pl.BlockSpec(memory_space=pltpu.VMEM)] * 2,
        scratch_shapes=[pltpu.SemaphoreType.DMA((2,))],
        compiler_params=pltpu.CompilerParams(vmem_limit_bytes=16 << 20),
        cost_estimate=pl.CostEstimate(flops=0, bytes_accessed=8 << 20, transcendentals=0),
    )(pltpu.with_memory_space_constraint(blocks, pltpu.HBM), pltpu.with_memory_space_constraint(basis, pltpu.HBM))


def add_products(table, count, blocks, basis, acc, transposed):
    live, spare = count[0, 0], acc.shape[0] - 1
    acc[...] = jnp.zeros_like(acc)

    def visit(step, carry):
        products, targets = [], []
        for u in range(UNROLL):
            s = step * UNROLL + u
            r, c = table[s] // 8, table[s] % 8
            source, target, dim = (r, c, 0) if transposed else (c, r, 1)
            products.append(
                lax.dot_general(
                    blocks[0, 0, s], basis[source], (((dim,), (0,)), ((), ())), preferred_element_type=F32
                )
            )
            targets.append(jnp.where(s < live, target, spare))
        for target, product in zip(targets, products):
            acc[target] += product
        return carry

    lax.fori_loop(0, (live + UNROLL - 1) // UNROLL, visit, 0)


def forward_kernel(table, count, blocks, *refs):
    pieces, (own, *sends), (basis, acc) = refs[:8], refs[8:12], refs[12:]
    y, k = lax.axis_index("row") // CORES, lax.axis_index("row") % CORES
    x = lax.axis_index("col") % NX
    for i, d in enumerate((0,) + SHIFTS_A):
        at = (y + 4 - d) % 4
        basis[at * CORES + k] = pieces[i][...]
        basis[at * CORES + 1 - k] = pieces[4 + i][...]
    add_products(table, count, blocks, basis, acc, False)
    for h in range(2):
        own[h] = acc[x * 2 + h]
    for send, d in zip(sends, SHIFTS_B):
        to = (x + d) % NX
        for h in range(2):
            send[h] = acc[to * 2 + h] * SCALE_X


def backward_kernel(table, count, blocks, *refs):
    pieces, (own, send), (basis, acc) = refs[:4], refs[4:6], refs[6:]
    k = lax.axis_index("row") % CORES
    x = lax.axis_index("col") % NX
    for i, d in enumerate((0,) + SHIFTS_C):
        at = (x + 4 - d) % 4
        for h in range(2):
            basis[at * 2 + h] = pieces[i][h]
    add_products(table, count, blocks, basis, acc, True)
    for y in range(4):
        own[y] = acc[y * CORES + k]
        send[y] = acc[y * CORES + 1 - k].astype(send.dtype)


def call(kernel, outs, scratch, n_vmem, *args):
    flops = 2 * 24 * 256**3
    return pl.pallas_call(
        kernel,
        out_shape=outs,
        in_specs=smem(2) + vmem(n_vmem),
        out_specs=vmem(len(outs)),
        scratch_shapes=scratch,
        compiler_params=pltpu.CompilerParams(vmem_limit_bytes=28 << 20),
        cost_estimate=pl.CostEstimate(flops=flops, bytes_accessed=1 << 20, transcendentals=0),
    )(*args)


def body(block_values, block_rows, block_cols, block_count, basis):
    n_row, n_col = lax.axis_size("row"), lax.axis_size("col")
    size, rank = basis.shape
    table = (block_rows[0, 0] * 8 + block_cols[0, 0], block_count)

    mine = [basis] + [lax.ppermute(basis, "row", shift_y(n_row, d)) for d in SHIFTS_A]
    blocks, own = fetch(block_values, basis)
    mine[1], blocks, own = lax.optimization_barrier((mine[1], blocks, own))
    other = [lax.ppermute(p, "row", swap_core(n_row)) for p in mine]
    own, *sends = call(
        forward_kernel,
        [jax.ShapeDtypeStruct((2, size, rank), F32)] * 4,
        [pltpu.VMEM((8, size, rank), BF16), pltpu.VMEM((9, size, rank), F32)],
        9,
        *table, blocks, own, *mine[1:], *other,
    )
    got = [lax.ppermute(s.astype(F16), "col", shift_x(n_col, d)) for d, s in zip(SHIFTS_B, sends)]
    x_sum = own + (got[0].astype(F32) + got[1].astype(F32) + got[2].astype(F32)) * (1 / SCALE_X)
    nz = n_col // NX
    parts = (x_sum * SCALE_Z).astype(F16).reshape(nz, 2 * size // nz, rank)
    parts = lax.all_to_all(parts, "col", 0, 0, tiled=True, axis_index_groups=z_groups(n_col))
    share = (jnp.sum(parts.astype(F32), axis=0) * (1 / SCALE_Z)).astype(BF16)

    copies = jnp.broadcast_to(share[None], (nz, *share.shape))
    chunk = lax.all_to_all(copies, "col", 0, 0, tiled=True, axis_index_groups=z_groups(n_col))
    chunk = chunk.reshape(2, size, rank)
    chunks = [chunk] + [lax.ppermute(chunk, "col", shift_x(n_col, d)) for d in SHIFTS_C]
    own, send = call(
        backward_kernel,
        [jax.ShapeDtypeStruct((4, size, rank), F32), jax.ShapeDtypeStruct((4, size, rank), BF16)],
        [pltpu.VMEM((8, size, rank), BF16), pltpu.VMEM((9, size, rank), F32)],
        5,
        *table, blocks, *chunks,
    )
    pair = own + lax.ppermute(send, "row", swap_core(n_row)).astype(F32)
    y = lax.axis_index("row") // CORES
    pick = lambda d: lax.dynamic_index_in_dim(pair, (y + d) % 4, 0, keepdims=False)
    got = [lax.ppermute(pick(d).astype(BF16), "row", shift_y(n_row, d)) for d in SHIFTS_D]
    return pick(0) + got[0].astype(F32) + got[1].astype(F32) + got[2].astype(F32)


def solution(mesh):
    in_specs = (
        P("row", "col", None, None, None),
        P("row", "col", None),
        P("row", "col", None),
        P("row", "col"),
        P(("col", "row"), None),
    )
    out_specs = P(("col", "row"), None)
    return jax.shard_map(body, mesh=mesh, in_specs=in_specs, out_specs=out_specs, check_vma=False)
```

```python
import jax
import jax.numpy as jnp
from jax import lax
from jax.experimental import pallas as pl
from jax.experimental.pallas import tpu as pltpu
from jax.sharding import PartitionSpec as P

BF16 = jnp.bfloat16
F32 = jnp.float32
F16 = jnp.float16
CORES = 2
NX = 4
UNROLL = 8
SHIFTS_A, SHIFTS_B, SHIFTS_C, SHIFTS_D = (1, 3, 2), (1, 3, 2), (1, 3, 2), (1, 3, 2)
TOP = 13.0
LEAST = -100.0
EXTRA = 8


def shift_y(count, d):
    ny = count // CORES
    return [(y * CORES + k, (y + d) % ny * CORES + k) for y in range(ny) for k in range(CORES)]


def swap_core(count):
    return [(i, i ^ 1) for i in range(count)]


def shift_x(count, d):
    return [(i, i // NX * NX + (i % NX + d) % NX) for i in range(count)]


def z_groups(count):
    return [[z * NX + x for z in range(count // NX)] for x in range(NX)]


def x_groups(count):
    return [[z * NX + x for x in range(NX)] for z in range(count // NX)]


def y_groups(count):
    return [[y * CORES + k for y in range(count // CORES)] for k in range(CORES)]


def vmem(n):
    return [pl.BlockSpec(memory_space=pltpu.VMEM)] * n


def smem(n):
    return [pl.BlockSpec(memory_space=pltpu.SMEM)] * n


def fetch_kernel(blocks, basis, blocks_out, basis_out, sems):
    copies = [
        pltpu.make_async_copy(blocks, blocks_out, sems.at[0]),
        pltpu.make_async_copy(basis, basis_out, sems.at[1]),
    ]
    for copy in copies:
        copy.start()
    for copy in copies:
        copy.wait()


def fetch(blocks, basis):
    return pl.pallas_call(
        fetch_kernel,
        out_shape=[jax.ShapeDtypeStruct(blocks.shape, blocks.dtype), jax.ShapeDtypeStruct(basis.shape, basis.dtype)],
        in_specs=[pl.BlockSpec(memory_space=pltpu.HBM)] * 2,
        out_specs=[pl.BlockSpec(memory_space=pltpu.VMEM)] * 2,
        scratch_shapes=[pltpu.SemaphoreType.DMA((2,))],
        compiler_params=pltpu.CompilerParams(vmem_limit_bytes=16 << 20),
        cost_estimate=pl.CostEstimate(flops=0, bytes_accessed=8 << 20, transcendentals=0),
    )(pltpu.with_memory_space_constraint(blocks, pltpu.HBM), pltpu.with_memory_space_constraint(basis, pltpu.HBM))


def add_products(table, count, blocks, basis, acc, transposed):
    live, spare = count[0, 0], acc.shape[0] - 1
    acc[...] = jnp.zeros_like(acc)

    def visit(step, carry):
        products, targets = [], []
        for u in range(UNROLL):
            s = step * UNROLL + u
            r, c = table[s] // 8, table[s] % 8
            source, target, dim = (r, c, 0) if transposed else (c, r, 1)
            products.append(
                lax.dot_general(
                    blocks[0, 0, s], basis[source], (((dim,), (0,)), ((), ())), preferred_element_type=F32
                )
            )
            targets.append(jnp.where(s < live, target, spare))
        for target, product in zip(targets, products):
            acc[target] += product
        return carry

    lax.fori_loop(0, (live + UNROLL - 1) // UNROLL, visit, 0)


def forward_kernel(table, count, blocks, *refs):
    pieces, (own_exponent, own, *sends), (basis, acc) = refs[:8], refs[8:13], refs[13:]
    y, k = lax.axis_index("row") // CORES, lax.axis_index("row") % CORES
    x = lax.axis_index("col") % NX
    for i, d in enumerate((0,) + SHIFTS_A):
        at = (y + 4 - d) % 4
        basis[at * CORES + k] = pieces[i][...]
        basis[at * CORES + 1 - k] = pieces[4 + i][...]
    add_products(table, count, blocks, basis, acc, False)
    largest = jnp.abs(acc[0])
    for r in range(1, 8):
        largest = jnp.maximum(largest, jnp.abs(acc[r]))
    largest = jnp.max(jnp.max(largest, axis=0, keepdims=True), axis=1, keepdims=True)
    exponent = jnp.maximum(jnp.ceil(jnp.log2(jnp.maximum(largest, 2.0**LEAST))), LEAST)
    scale = jnp.exp2(TOP - exponent)
    own_exponent[...] = jnp.broadcast_to(exponent, own_exponent.shape)
    size = acc.shape[1]
    for h in range(2):
        own[h] = acc[x * 2 + h]
    for send, d in zip(sends, SHIFTS_B):
        to = (x + d) % NX
        for h in range(2):
            send[h * size : (h + 1) * size] = acc[to * 2 + h] * scale
        send[2 * size :] = jnp.broadcast_to(exponent, (EXTRA, send.shape[1]))


def backward_kernel(table, count, blocks, *refs):
    pieces, (own, send), (basis, acc) = refs[:4], refs[4:6], refs[6:]
    k = lax.axis_index("row") % CORES
    x = lax.axis_index("col") % NX
    for i, d in enumerate((0,) + SHIFTS_C):
        at = (x + 4 - d) % 4
        for h in range(2):
            basis[at * 2 + h] = pieces[i][h]
    add_products(table, count, blocks, basis, acc, True)
    for y in range(4):
        own[y] = acc[y * CORES + k]
        send[y] = acc[y * CORES + 1 - k].astype(send.dtype)


def call(kernel, outs, scratch, n_vmem, *args):
    flops = 2 * 24 * 256**3
    return pl.pallas_call(
        kernel,
        out_shape=outs,
        in_specs=smem(2) + vmem(n_vmem),
        out_specs=vmem(len(outs)),
        scratch_shapes=scratch,
        compiler_params=pltpu.CompilerParams(vmem_limit_bytes=28 << 20),
        cost_estimate=pl.CostEstimate(flops=flops, bytes_accessed=1 << 20, transcendentals=0),
    )(*args)


def body(block_values, block_rows, block_cols, block_count, basis):
    n_row, n_col = lax.axis_size("row"), lax.axis_size("col")
    size, rank = basis.shape
    table = (block_rows[0, 0] * 8 + block_cols[0, 0], block_count)

    mine = [basis] + [lax.ppermute(basis, "row", shift_y(n_row, d)) for d in SHIFTS_A]
    blocks, own = fetch(block_values, basis)
    mine[1], blocks, own = lax.optimization_barrier((mine[1], blocks, own))
    other = [lax.ppermute(p, "row", swap_core(n_row)) for p in mine]
    exponent, own, *sends = call(
        forward_kernel,
        [
            jax.ShapeDtypeStruct((EXTRA, rank), F32),
            jax.ShapeDtypeStruct((2, size, rank), F32),
            *[jax.ShapeDtypeStruct((2 * size + EXTRA, rank), F32)] * 3,
        ],
        [pltpu.VMEM((8, size, rank), BF16), pltpu.VMEM((9, size, rank), F32)],
        9,
        *table, blocks, own, *mine[1:], *other,
    )
    got = [lax.ppermute(s.astype(F16), "col", shift_x(n_col, d)) for d, s in zip(SHIFTS_B, sends)]
    x_sum = own.reshape(2 * size, rank)
    exponent = exponent[:1]
    for piece in got:
        theirs = piece[2 * size : 2 * size + 1].astype(F32)
        x_sum += piece[: 2 * size].astype(F32) * jnp.exp2(theirs - TOP)
        exponent = jnp.maximum(exponent, theirs)
    exponent = exponent + 2
    nz = n_col // NX
    rows = 2 * size // nz
    parts = (x_sum * jnp.exp2(TOP - exponent)).astype(F16).reshape(nz, rows, rank)
    parts = jnp.concatenate([parts, jnp.broadcast_to(exponent.astype(F16), (nz, EXTRA, rank))], 1)
    parts = lax.all_to_all(parts, "col", 0, 0, tiled=True, axis_index_groups=z_groups(n_col))
    scale = jnp.exp2(parts[:, rows : rows + 1].astype(F32) - TOP)
    share = jnp.sum(parts[:, :rows].astype(F32) * scale, axis=0).astype(BF16)

    copies = jnp.broadcast_to(share[None], (nz, *share.shape))
    chunk = lax.all_to_all(copies, "col", 0, 0, tiled=True, axis_index_groups=z_groups(n_col))
    chunk = chunk.reshape(2, size, rank)
    chunks = [chunk] + [lax.ppermute(chunk, "col", shift_x(n_col, d)) for d in SHIFTS_C]
    own, send = call(
        backward_kernel,
        [jax.ShapeDtypeStruct((4, size, rank), F32), jax.ShapeDtypeStruct((4, size, rank), BF16)],
        [pltpu.VMEM((8, size, rank), BF16), pltpu.VMEM((9, size, rank), F32)],
        5,
        *table, blocks, *chunks,
    )
    pair = own + lax.ppermute(send, "row", swap_core(n_row)).astype(F32)
    y = lax.axis_index("row") // CORES
    pick = lambda d: lax.dynamic_index_in_dim(pair, (y + d) % 4, 0, keepdims=False)
    got = [lax.ppermute(pick(d).astype(BF16), "row", shift_y(n_row, d)) for d in SHIFTS_D]
    return pick(0) + got[0].astype(F32) + got[1].astype(F32) + got[2].astype(F32)


def solution(mesh):
    in_specs = (
        P("row", "col", None, None, None),
        P("row", "col", None),
        P("row", "col", None),
        P("row", "col"),
        P(("col", "row"), None),
    )
    out_specs = P(("col", "row"), None)
    return jax.shard_map(body, mesh=mesh, in_specs=in_specs, out_specs=out_specs, check_vma=False)
```

```python
import jax
import jax.numpy as jnp
from jax import lax
from jax.experimental import pallas as pl
from jax.experimental.pallas import tpu as pltpu
from jax.sharding import PartitionSpec as P

BF16 = jnp.bfloat16
F32 = jnp.float32
F16 = jnp.float16
CORES = 2
NX = 4
UNROLL = 12
SHIFTS_A, SHIFTS_B, SHIFTS_C, SHIFTS_D = (1, 3, 2), (1, 3, 2), (1, 3, 2), (1, 3, 2)
TOP = 13.0
LEAST = -100.0
EXTRA = 8


def shift_y(count, d):
    ny = count // CORES
    return [(y * CORES + k, (y + d) % ny * CORES + k) for y in range(ny) for k in range(CORES)]


def swap_core(count):
    return [(i, i ^ 1) for i in range(count)]


def shift_x(count, d):
    return [(i, i // NX * NX + (i % NX + d) % NX) for i in range(count)]


def z_groups(count):
    return [[z * NX + x for z in range(count // NX)] for x in range(NX)]


def x_groups(count):
    return [[z * NX + x for x in range(NX)] for z in range(count // NX)]


def y_groups(count):
    return [[y * CORES + k for y in range(count // CORES)] for k in range(CORES)]


def vmem(n):
    return [pl.BlockSpec(memory_space=pltpu.VMEM)] * n


def smem(n):
    return [pl.BlockSpec(memory_space=pltpu.SMEM)] * n


def fetch_kernel(blocks, basis, blocks_out, basis_out, sems):
    copies = [
        pltpu.make_async_copy(blocks, blocks_out, sems.at[0]),
        pltpu.make_async_copy(basis, basis_out, sems.at[1]),
    ]
    for copy in copies:
        copy.start()
    for copy in copies:
        copy.wait()


def fetch(blocks, basis):
    return pl.pallas_call(
        fetch_kernel,
        out_shape=[jax.ShapeDtypeStruct(blocks.shape, blocks.dtype), jax.ShapeDtypeStruct(basis.shape, basis.dtype)],
        in_specs=[pl.BlockSpec(memory_space=pltpu.HBM)] * 2,
        out_specs=[pl.BlockSpec(memory_space=pltpu.VMEM)] * 2,
        scratch_shapes=[pltpu.SemaphoreType.DMA((2,))],
        compiler_params=pltpu.CompilerParams(vmem_limit_bytes=16 << 20),
        cost_estimate=pl.CostEstimate(flops=0, bytes_accessed=8 << 20, transcendentals=0),
    )(pltpu.with_memory_space_constraint(blocks, pltpu.HBM), pltpu.with_memory_space_constraint(basis, pltpu.HBM))


def add_products(table, count, blocks, basis, acc, transposed):
    live, spare = count[0, 0], acc.shape[0] - 1
    acc[...] = jnp.zeros_like(acc)

    def visit(step, carry):
        products, targets = [], []
        for u in range(UNROLL):
            s = step * UNROLL + u
            r, c = table[s] // 8, table[s] % 8
            source, target, dim = (r, c, 0) if transposed else (c, r, 1)
            products.append(
                lax.dot_general(
                    blocks[0, 0, s], basis[source], (((dim,), (0,)), ((), ())), preferred_element_type=F32
                )
            )
            targets.append(jnp.where(s < live, target, spare))
        for target, product in zip(targets, products):
            acc[target] += product
        return carry

    lax.fori_loop(0, (live + UNROLL - 1) // UNROLL, visit, 0)


def forward_kernel(table, count, blocks, *refs):
    pieces, (own_exponent, own, *sends), (basis, acc) = refs[:8], refs[8:13], refs[13:]
    y, k = lax.axis_index("row") // CORES, lax.axis_index("row") % CORES
    x = lax.axis_index("col") % NX
    for i, d in enumerate((0,) + SHIFTS_A):
        at = (y + 4 - d) % 4
        basis[at * CORES + k] = pieces[i][...]
        basis[at * CORES + 1 - k] = pieces[4 + i][...]
    add_products(table, count, blocks, basis, acc, False)
    largest = jnp.abs(acc[0])
    for r in range(1, 8):
        largest = jnp.maximum(largest, jnp.abs(acc[r]))
    largest = jnp.max(jnp.max(largest, axis=0, keepdims=True), axis=1, keepdims=True)
    exponent = jnp.maximum(jnp.ceil(jnp.log2(jnp.maximum(largest, 2.0**LEAST))), LEAST)
    scale = jnp.exp2(TOP - exponent)
    own_exponent[...] = jnp.broadcast_to(exponent, own_exponent.shape)
    size = acc.shape[1]
    for h in range(2):
        own[h] = acc[x * 2 + h]
    for send, d in zip(sends, SHIFTS_B):
        to = (x + d) % NX
        for h in range(2):
            send[h * size : (h + 1) * size] = acc[to * 2 + h] * scale
        send[2 * size :] = jnp.broadcast_to(exponent, (EXTRA, send.shape[1]))


def backward_kernel(table, count, blocks, *refs):
    pieces, (own, send), (basis, acc) = refs[:4], refs[4:6], refs[6:]
    k = lax.axis_index("row") % CORES
    x = lax.axis_index("col") % NX
    for i, d in enumerate((0,) + SHIFTS_C):
        at = (x + 4 - d) % 4
        for h in range(2):
            basis[at * 2 + h] = pieces[i][h]
    add_products(table, count, blocks, basis, acc, True)
    for y in range(4):
        own[y] = acc[y * CORES + k]
        send[y] = acc[y * CORES + 1 - k].astype(send.dtype)


def call(kernel, outs, scratch, n_vmem, *args):
    flops = 2 * 24 * 256**3
    return pl.pallas_call(
        kernel,
        out_shape=outs,
        in_specs=smem(2) + vmem(n_vmem),
        out_specs=vmem(len(outs)),
        scratch_shapes=scratch,
        compiler_params=pltpu.CompilerParams(vmem_limit_bytes=28 << 20),
        cost_estimate=pl.CostEstimate(flops=flops, bytes_accessed=1 << 20, transcendentals=0),
    )(*args)


def body(block_values, block_rows, block_cols, block_count, basis):
    n_row, n_col = lax.axis_size("row"), lax.axis_size("col")
    size, rank = basis.shape
    table = (block_rows[0, 0] * 8 + block_cols[0, 0], block_count)

    mine = [basis] + [lax.ppermute(basis, "row", shift_y(n_row, d)) for d in SHIFTS_A]
    blocks, own = fetch(block_values, basis)
    mine[1], blocks, own = lax.optimization_barrier((mine[1], blocks, own))
    other = [lax.ppermute(p, "row", swap_core(n_row)) for p in mine]
    exponent, own, *sends = call(
        forward_kernel,
        [
            jax.ShapeDtypeStruct((EXTRA, rank), F32),
            jax.ShapeDtypeStruct((2, size, rank), F32),
            *[jax.ShapeDtypeStruct((2 * size + EXTRA, rank), F32)] * 3,
        ],
        [pltpu.VMEM((8, size, rank), BF16), pltpu.VMEM((9, size, rank), F32)],
        9,
        *table, blocks, own, *mine[1:], *other,
    )
    got = [lax.ppermute(s.astype(F16), "col", shift_x(n_col, d)) for d, s in zip(SHIFTS_B, sends)]
    x_sum = own.reshape(2 * size, rank)
    exponent = exponent[:1]
    for piece in got:
        theirs = piece[2 * size : 2 * size + 1].astype(F32)
        x_sum += piece[: 2 * size].astype(F32) * jnp.exp2(theirs - TOP)
        exponent = jnp.maximum(exponent, theirs)
    exponent = exponent + 2
    nz = n_col // NX
    rows = 2 * size // nz
    parts = (x_sum * jnp.exp2(TOP - exponent)).astype(F16).reshape(nz, rows, rank)
    parts = jnp.concatenate([parts, jnp.broadcast_to(exponent.astype(F16), (nz, EXTRA, rank))], 1)
    parts = lax.all_to_all(parts, "col", 0, 0, tiled=True, axis_index_groups=z_groups(n_col))
    scale = jnp.exp2(parts[:, rows : rows + 1].astype(F32) - TOP)
    share = jnp.sum(parts[:, :rows].astype(F32) * scale, axis=0).astype(BF16)

    copies = jnp.broadcast_to(share[None], (nz, *share.shape))
    chunk = lax.all_to_all(copies, "col", 0, 0, tiled=True, axis_index_groups=z_groups(n_col))
    chunk = chunk.reshape(2, size, rank)
    chunks = [chunk] + [lax.ppermute(chunk, "col", shift_x(n_col, d)) for d in SHIFTS_C]
    own, send = call(
        backward_kernel,
        [jax.ShapeDtypeStruct((4, size, rank), F32), jax.ShapeDtypeStruct((4, size, rank), BF16)],
        [pltpu.VMEM((8, size, rank), BF16), pltpu.VMEM((9, size, rank), F32)],
        5,
        *table, blocks, *chunks,
    )
    pair = own + lax.ppermute(send, "row", swap_core(n_row)).astype(F32)
    y = lax.axis_index("row") // CORES
    pick = lambda d: lax.dynamic_index_in_dim(pair, (y + d) % 4, 0, keepdims=False)
    got = [lax.ppermute(pick(d).astype(BF16), "row", shift_y(n_row, d)) for d in SHIFTS_D]
    return pick(0) + got[0].astype(F32) + got[1].astype(F32) + got[2].astype(F32)


def solution(mesh):
    in_specs = (
        P("row", "col", None, None, None),
        P("row", "col", None),
        P("row", "col", None),
        P("row", "col"),
        P(("col", "row"), None),
    )
    out_specs = P(("col", "row"), None)
    return jax.shard_map(body, mesh=mesh, in_specs=in_specs, out_specs=out_specs, check_vma=False)
```

```python
import jax
import jax.numpy as jnp
from jax import lax
from jax.experimental import pallas as pl
from jax.experimental.pallas import tpu as pltpu
from jax.sharding import PartitionSpec as P

BF16 = jnp.bfloat16
F32 = jnp.float32
F16 = jnp.float16
CORES = 2
NX = 4
UNROLL = 8
SHIFTS_A, SHIFTS_B, SHIFTS_C, SHIFTS_D = (1, 3, 2), (1, 3, 2), (2, 1, 3), (2, 1, 3)
TOP = 13.0
LEAST = -100.0
EXTRA = 8


def shift_y(count, d):
    ny = count // CORES
    return [(y * CORES + k, (y + d) % ny * CORES + k) for y in range(ny) for k in range(CORES)]


def swap_core(count):
    return [(i, i ^ 1) for i in range(count)]


def shift_x(count, d):
    return [(i, i // NX * NX + (i % NX + d) % NX) for i in range(count)]


def z_groups(count):
    return [[z * NX + x for z in range(count // NX)] for x in range(NX)]


def x_groups(count):
    return [[z * NX + x for x in range(NX)] for z in range(count // NX)]


def y_groups(count):
    return [[y * CORES + k for y in range(count // CORES)] for k in range(CORES)]


def vmem(n):
    return [pl.BlockSpec(memory_space=pltpu.VMEM)] * n


def smem(n):
    return [pl.BlockSpec(memory_space=pltpu.SMEM)] * n


def fetch_kernel(blocks, basis, blocks_out, basis_out, sems):
    copies = [
        pltpu.make_async_copy(blocks, blocks_out, sems.at[0]),
        pltpu.make_async_copy(basis, basis_out, sems.at[1]),
    ]
    for copy in copies:
        copy.start()
    for copy in copies:
        copy.wait()


def fetch(blocks, basis):
    return pl.pallas_call(
        fetch_kernel,
        out_shape=[jax.ShapeDtypeStruct(blocks.shape, blocks.dtype), jax.ShapeDtypeStruct(basis.shape, basis.dtype)],
        in_specs=[pl.BlockSpec(memory_space=pltpu.HBM)] * 2,
        out_specs=[pl.BlockSpec(memory_space=pltpu.VMEM)] * 2,
        scratch_shapes=[pltpu.SemaphoreType.DMA((2,))],
        compiler_params=pltpu.CompilerParams(vmem_limit_bytes=16 << 20),
        cost_estimate=pl.CostEstimate(flops=0, bytes_accessed=8 << 20, transcendentals=0),
    )(pltpu.with_memory_space_constraint(blocks, pltpu.HBM), pltpu.with_memory_space_constraint(basis, pltpu.HBM))


def add_products(table, count, blocks, basis, acc, transposed):
    live, spare = count[0, 0], acc.shape[0] - 1
    acc[...] = jnp.zeros_like(acc)

    def visit(step, carry):
        products, targets = [], []
        for u in range(UNROLL):
            s = step * UNROLL + u
            r, c = table[s] // 8, table[s] % 8
            source, target, dim = (r, c, 0) if transposed else (c, r, 1)
            products.append(
                lax.dot_general(
                    blocks[0, 0, s], basis[source], (((dim,), (0,)), ((), ())), preferred_element_type=F32
                )
            )
            targets.append(jnp.where(s < live, target, spare))
        for target, product in zip(targets, products):
            acc[target] += product
        return carry

    lax.fori_loop(0, (live + UNROLL - 1) // UNROLL, visit, 0)


def forward_kernel(table, count, blocks, *refs):
    pieces, (own_exponent, own, *sends), (basis, acc) = refs[:8], refs[8:13], refs[13:]
    y, k = lax.axis_index("row") // CORES, lax.axis_index("row") % CORES
    x = lax.axis_index("col") % NX
    for i, d in enumerate((0,) + SHIFTS_A):
        at = (y + 4 - d) % 4
        basis[at * CORES + k] = pieces[i][...]
        basis[at * CORES + 1 - k] = pieces[4 + i][...]
    add_products(table, count, blocks, basis, acc, False)
    largest = jnp.abs(acc[0])
    for r in range(1, 8):
        largest = jnp.maximum(largest, jnp.abs(acc[r]))
    largest = jnp.max(jnp.max(largest, axis=0, keepdims=True), axis=1, keepdims=True)
    exponent = jnp.maximum(jnp.ceil(jnp.log2(jnp.maximum(largest, 2.0**LEAST))), LEAST)
    scale = jnp.exp2(TOP - exponent)
    own_exponent[...] = jnp.broadcast_to(exponent, own_exponent.shape)
    size = acc.shape[1]
    for h in range(2):
        own[h] = acc[x * 2 + h]
    for send, d in zip(sends, SHIFTS_B):
        to = (x + d) % NX
        for h in range(2):
            send[h * size : (h + 1) * size] = acc[to * 2 + h] * scale
        send[2 * size :] = jnp.broadcast_to(exponent, (EXTRA, send.shape[1]))


def backward_kernel(table, count, blocks, *refs):
    pieces, (own, send), (basis, acc) = refs[:4], refs[4:6], refs[6:]
    k = lax.axis_index("row") % CORES
    x = lax.axis_index("col") % NX
    for i, d in enumerate((0,) + SHIFTS_C):
        at = (x + 4 - d) % 4
        for h in range(2):
            basis[at * 2 + h] = pieces[i][h]
    add_products(table, count, blocks, basis, acc, True)
    for y in range(4):
        own[y] = acc[y * CORES + k]
        send[y] = acc[y * CORES + 1 - k].astype(send.dtype)


def call(kernel, outs, scratch, n_vmem, *args):
    flops = 2 * 24 * 256**3
    return pl.pallas_call(
        kernel,
        out_shape=outs,
        in_specs=smem(2) + vmem(n_vmem),
        out_specs=vmem(len(outs)),
        scratch_shapes=scratch,
        compiler_params=pltpu.CompilerParams(vmem_limit_bytes=28 << 20),
        cost_estimate=pl.CostEstimate(flops=flops, bytes_accessed=1 << 20, transcendentals=0),
    )(*args)


def body(block_values, block_rows, block_cols, block_count, basis):
    n_row, n_col = lax.axis_size("row"), lax.axis_size("col")
    size, rank = basis.shape
    table = (block_rows[0, 0] * 8 + block_cols[0, 0], block_count)

    mine = [basis] + [lax.ppermute(basis, "row", shift_y(n_row, d)) for d in SHIFTS_A]
    blocks, own = fetch(block_values, basis)
    mine[1], blocks, own = lax.optimization_barrier((mine[1], blocks, own))
    other = [lax.ppermute(p, "row", swap_core(n_row)) for p in mine]
    exponent, own, *sends = call(
        forward_kernel,
        [
            jax.ShapeDtypeStruct((EXTRA, rank), F32),
            jax.ShapeDtypeStruct((2, size, rank), F32),
            *[jax.ShapeDtypeStruct((2 * size + EXTRA, rank), F32)] * 3,
        ],
        [pltpu.VMEM((8, size, rank), BF16), pltpu.VMEM((9, size, rank), F32)],
        9,
        *table, blocks, own, *mine[1:], *other,
    )
    got = [lax.ppermute(s.astype(F16), "col", shift_x(n_col, d)) for d, s in zip(SHIFTS_B, sends)]
    x_sum = own.reshape(2 * size, rank)
    exponent = exponent[:1]
    for piece in got:
        theirs = piece[2 * size : 2 * size + 1].astype(F32)
        x_sum += piece[: 2 * size].astype(F32) * jnp.exp2(theirs - TOP)
        exponent = jnp.maximum(exponent, theirs)
    exponent = exponent + 2
    nz = n_col // NX
    rows = 2 * size // nz
    parts = (x_sum * jnp.exp2(TOP - exponent)).astype(F16).reshape(nz, rows, rank)
    parts = jnp.concatenate([parts, jnp.broadcast_to(exponent.astype(F16), (nz, EXTRA, rank))], 1)
    parts = lax.all_to_all(parts, "col", 0, 0, tiled=True, axis_index_groups=z_groups(n_col))
    scale = jnp.exp2(parts[:, rows : rows + 1].astype(F32) - TOP)
    share = jnp.sum(parts[:, :rows].astype(F32) * scale, axis=0).astype(BF16)

    copies = jnp.broadcast_to(share[None], (nz, *share.shape))
    chunk = lax.all_to_all(copies, "col", 0, 0, tiled=True, axis_index_groups=z_groups(n_col))
    chunk = chunk.reshape(2, size, rank)
    chunks = [chunk] + [lax.ppermute(chunk, "col", shift_x(n_col, d)) for d in SHIFTS_C]
    own, send = call(
        backward_kernel,
        [jax.ShapeDtypeStruct((4, size, rank), F32), jax.ShapeDtypeStruct((4, size, rank), BF16)],
        [pltpu.VMEM((8, size, rank), BF16), pltpu.VMEM((9, size, rank), F32)],
        5,
        *table, blocks, *chunks,
    )
    pair = own + lax.ppermute(send, "row", swap_core(n_row)).astype(F32)
    y = lax.axis_index("row") // CORES
    pick = lambda d: lax.dynamic_index_in_dim(pair, (y + d) % 4, 0, keepdims=False)
    got = [lax.ppermute(pick(d).astype(BF16), "row", shift_y(n_row, d)) for d in SHIFTS_D]
    return pick(0) + got[0].astype(F32) + got[1].astype(F32) + got[2].astype(F32)


def solution(mesh):
    in_specs = (
        P("row", "col", None, None, None),
        P("row", "col", None),
        P("row", "col", None),
        P("row", "col"),
        P(("col", "row"), None),
    )
    out_specs = P(("col", "row"), None)
    return jax.shard_map(body, mesh=mesh, in_specs=in_specs, out_specs=out_specs, check_vma=False)
```
